32 devices in a mesh: grp: 2 (over y), batch: 8 (over z, x), tensor: 2 (over core).
Axes of the slice: x: 2, y: 2, z: 4, core: 2. Of those that a mesh axis runs over, the one named last changes fastest.
Arguments:
- init_cache: bfloat16 [16, 2, 64, 3072], P(('grp', 'batch'), None, None, 'tensor'), parts along dimension 0, may hold values from -6 to 6
- memory: bfloat16 [16, 2, 64, 3072], P(('grp', 'batch'), None, None, 'tensor'), parts along dimension 0, may hold values from -6 to 6
- queries: bfloat16 [1, 16, 2, 3072], P(None, ('grp', 'batch'), None, 'tensor'), parts along dimension 1, may hold values from -600 to 600
- new_kv: bfloat16 [1, 16, 2, 3072], P(None, ('grp', 'batch'), None, 'tensor'), parts along dimension 1, may hold values from -6 to 6
- residual: bfloat16 [1, 16, 6144], P(None, 'grp', 'batch'), parts along dimension 1, may hold values from -6 to 6
- out_weight: bfloat16 [2, 3072, 6144], P(None, 'tensor', 'batch'), may hold values from -0.078125 to 0.078125
- up_weight: bfloat16 [6144, 24576], P(None, ('batch', 'tensor')), may hold values from -0.078125 to 0.078125
- down_weight: bfloat16 [24576, 6144], P('batch', 'tensor'), may hold values from -0.0390625 to 0.0390625
- parents: int32 [1, 16], P(None, 'grp'), parts along dimension 1, may hold values from 0 to 7
- lengths: int32 [2], P('grp'), parts along dimension 0, may hold values from 1 to 63
Outputs:
- hidden: bfloat16 [1, 16, 6144], P(None, 'grp', 'batch'), parts along dimension 1
- ffn_out: bfloat16 [1, 16, 6144], P(None, ('grp', 'batch'), 'tensor'), parts along dimension 1
- final_cache: bfloat16 [16, 2, 64, 3072], P(('grp', 'batch'), None, None, 'tensor'), parts along dimension 0
The draws below stay inside these ranges and needn't reach their ends.
There are 2 independent parts, one for each index of `grp`. The reference program is written for one: setup_inputs(seed, part) draws one part's arguments, and reference() takes and returns one part's arrays. A program takes and returns all parts, laid end to end along the dimension named above; an argument that names none is the same for every part. Nothing has to cross between parts.
Inputs may be any that keep to these rules, and one draw needn't show every extreme that they name: parents[s, b + r] is the beam of request r whose cache beam b continues at step s.
All inputs are finite; a program needn't handle non-finite values.
Results may differ from the reference program's by a relative error of at most 0.006.
Values may be sent and summed in bfloat16 or wider, within the bound.
A program may use at most 128 MiB of HBM per device.

```python
import math
import jax
import jax.numpy as jnp
from jax import lax

D = 6144
HEADS = 24
HD = 128
FF = 24576
BEAMS = 8
STEPS = 1
CACHE = 64
FB = 64
HF = 3072
ROWS = 8
REQ = 1


def draw_queries(key, part):
    base = jax.random.truncated_normal(key, -6.0, 6.0, (STEPS, ROWS, 2, HF), jnp.float32)
    return base.astype(jnp.bfloat16)


def with_ends(result, stream_key, least, largest):
    longest = result.shape.index(max(result.shape))
    spots = []
    for shift in (0, 1):
        where = [jax.random.randint(jax.random.fold_in(stream_key, axis), (), 0, length) for axis, length in enumerate(result.shape)]
        where[longest] = (where[longest] + shift) % result.shape[longest]
        spots.append(tuple(where))
    return result.at[spots[0]].set(least).at[spots[1]].set(largest)


def block_scale(stream_key, dims, split, least, largest):
    level, own = 1.0, jax.random.fold_in(stream_key, 6)
    for dim, parts in split:
        draws = jnp.exp(jax.random.uniform(jax.random.fold_in(own, dim), (parts,), jnp.float32, least / len(split), largest / len(split)))
        level = level * jnp.repeat(draws, dims[dim] // parts).reshape([-1 if axis == dim else 1 for axis in range(len(dims))])
    return level


def scatter_about(rng, dims, deviation, most, shards=(), kind=jnp.bfloat16):
    drawn = deviation * jax.random.normal(rng, dims, jnp.float32)
    if shards:
        drawn = drawn * block_scale(rng, dims, shards, -0.22, 0.18)
    return jnp.clip(drawn, -most, most).astype(kind)


def setup_inputs(seed: int = 0, part: int = 0) -> dict:
    key_list = jax.random.split(jax.random.key(seed), 11)
    part_splits = jax.random.split(jax.random.fold_in(key_list[10], part), 11)
    init_cache = scatter_about(part_splits[0], (ROWS, 2, CACHE, HF), 1.0, 6.0, ((0, 8), (3, 2)))
    memory = scatter_about(part_splits[1], (ROWS, 2, FB, HF), 1.0, 6.0, ((0, 8), (3, 2)))
    queries = draw_queries(jax.random.fold_in(jax.random.fold_in(key_list[10], part), 71), part)
    new_kv = scatter_about(part_splits[3], (STEPS, ROWS, 2, HF), 1.0, 6.0, ((1, 8), (3, 2)))
    residual = scatter_about(part_splits[4], (STEPS, ROWS, D), 1.0, 6.0, ((2, 8),))
    out_weight = scatter_about(key_list[5], (2, HF, D), (2 * HF) ** -0.5, 0.078125, ((1, 2), (2, 8)))
    up_weight = scatter_about(key_list[6], (D, FF), D ** -0.5, 0.078125, ((1, 16),))
    down_weight = scatter_about(key_list[7], (FF, D), FF ** -0.5, 0.0390625, ((0, 8), (1, 2)))
    parents = with_ends(jax.random.randint(part_splits[8], (STEPS, ROWS), 0, BEAMS), jax.random.fold_in(part_splits[8], 1), 0, BEAMS - 1).astype(jnp.int32)
    lengths = jax.random.randint(part_splits[9], (REQ,), 1, CACHE - STEPS + 1).astype(jnp.int32)
    return {"init_cache": init_cache, "memory": memory, "queries": queries, "new_kv": new_kv, "residual": residual, "out_weight": out_weight, "up_weight": up_weight, "down_weight": down_weight, "parents": parents, "lengths": lengths}


def reference(init_cache, memory, queries, new_kv, residual, out_weight, up_weight, down_weight, parents, lengths):
    highest = lax.Precision.HIGHEST
    row_request = jnp.arange(ROWS, dtype=jnp.int32) % REQ
    slots = jnp.arange(CACHE, dtype=jnp.int32)
    row_length = lengths[row_request]
    mem = memory.astype(jnp.float32).reshape(BEAMS, REQ, 2, FB, HEADS, HD)
    mem_keys = mem[:, :, 0].transpose(1, 0, 2, 3, 4).reshape(REQ, BEAMS * FB, HEADS, HD)
    mem_values = mem[:, :, 1].transpose(1, 0, 2, 3, 4).reshape(REQ, BEAMS * FB, HEADS, HD)
    cache = init_cache
    hidden_list = []
    ffn_list = []
    for step in range(STEPS):
        source = (parents[step] * REQ + row_request).astype(jnp.int32)
        cache = cache[source]
        write = slots[None, :] == (row_length + step)[:, None]
        cache = jnp.where(write[:, None, :, None], new_kv[step][:, :, None, :], cache)
        query_all = queries[step].astype(jnp.float32)
        self_query = query_all[:, 0].reshape(ROWS, HEADS, HD)
        keys = cache[:, 0].astype(jnp.float32).reshape(ROWS, CACHE, HEADS, HD)
        values = cache[:, 1].astype(jnp.float32).reshape(ROWS, CACHE, HEADS, HD)
        scores = jnp.einsum('rhd,rchd->rhc', self_query, keys, precision=highest) / math.sqrt(HD)
        valid = (slots[None, :] <= (row_length + step)[:, None])[:, None, :]
        masked = jnp.where(valid, scores, -1e+30)
        peak = lax.optimization_barrier(jnp.max(masked, axis=-1, keepdims=True))
        weights = jnp.where(valid, jnp.exp(masked - peak), 0.0)
        total = lax.optimization_barrier(jnp.sum(weights, axis=-1))
        weighted = jnp.einsum('rhc,rchd->rhd', weights, values, precision=highest)
        self_out = (weighted / total[..., None]).reshape(ROWS, HF).astype(jnp.bfloat16)
        cross_query = query_all[:, 1].reshape(BEAMS, REQ, HEADS, HD)
        scores = jnp.einsum('brhd,rfhd->brhf', cross_query, mem_keys, precision=highest) / math.sqrt(HD)
        peak = lax.optimization_barrier(jnp.max(scores, axis=-1, keepdims=True))
        weights = jnp.exp(scores - peak)
        total = lax.optimization_barrier(jnp.sum(weights, axis=-1))
        weighted = jnp.einsum('brhf,rfhd->brhd', weights, mem_values, precision=highest)
        cross_out = (weighted / total[..., None]).reshape(ROWS, HF).astype(jnp.bfloat16)
        attended = jnp.stack([self_out, cross_out], axis=1).reshape(ROWS, 2 * HF)
        projected = jnp.dot(attended, out_weight.reshape(2 * HF, D), preferred_element_type=jnp.float32)
        hidden = (residual[step].astype(jnp.float32) + projected).astype(jnp.bfloat16)
        pre_act = jnp.dot(hidden, up_weight, preferred_element_type=jnp.float32)
        activation = jax.nn.gelu(pre_act, approximate=False).astype(jnp.bfloat16)
        ffn_row = jnp.dot(activation, down_weight, preferred_element_type=jnp.float32).astype(jnp.bfloat16)
        hidden_list.append(hidden)
        ffn_list.append(ffn_row)
    return (jnp.stack(hidden_list), jnp.stack(ffn_list), cache)
```

```python
import math

import jax
import jax.numpy as jnp
from jax import lax
from jax.experimental import pallas as pl
from jax.experimental.pallas import tpu as pltpu
from jax.sharding import PartitionSpec as P

HD = 128
BEAMS = 8


def from_behind(value, axis, by):
    devices = lax.axis_size(axis)
    return lax.ppermute(value, axis, [(i, (i + by) % devices) for i in range(devices)])


def attend(query, keys, values, valid):
    highest = lax.Precision.HIGHEST
    scores = jnp.einsum("nhd,chd->nhc", query, keys, precision=highest) / math.sqrt(HD)
    mask = valid[:, None, :]
    masked = jnp.where(mask, scores, -1e30)
    peak = jnp.max(masked, axis=-1)
    weights = jnp.where(mask, jnp.exp(masked - peak[..., None]), 0.0)
    total = jnp.sum(weights, axis=-1)
    weighted = jnp.einsum("nhc,chd->nhd", weights, values, precision=highest)
    return (weighted, peak, total)


def spread(payload, stride):
    items = [payload]
    for offset in range(1, BEAMS):
        items.append(from_behind(payload, "batch", offset * stride))
    return jnp.stack(items)


def take_from(block, source, own_beam, stride):
    wanted = (own_beam - source) % BEAMS
    result = block
    for offset in range(1, BEAMS):
        moved = from_behind(block, "batch", offset * stride)
        result = jnp.where(wanted == offset, moved, result)
    return result


def collect(weighted, peak, total, stride):
    gathered = [(weighted[0], peak[0], total[0])]
    for offset in range(1, BEAMS):
        gathered.append(
            from_behind((weighted[offset], peak[offset], total[offset]), "batch", -offset * stride)
        )
    return gathered


def combine(gathered):
    peaks = jnp.stack([entry[1] for entry in gathered])
    top = jnp.max(peaks, axis=0)
    factors = jnp.exp(peaks - top[None])
    numer = jnp.sum(jnp.stack([entry[0] for entry in gathered]) * factors[..., None], axis=0)
    denom = jnp.sum(jnp.stack([entry[2] for entry in gathered]) * factors, axis=0)
    return numer / denom[..., None]


def body(
    init_cache,
    memory,
    queries,
    new_kv,
    residual,
    out_weight,
    up_weight,
    down_weight,
    parents,
    lengths,
):
    stride = lax.axis_size("batch") // BEAMS
    position = lax.axis_index("batch")
    own_beam = position // stride
    request = position % stride
    width_local = queries.shape[-1]
    local_heads = width_local // HD
    cache_len = init_cache.shape[2]
    steps = queries.shape[0]
    request_ids = jnp.arange(stride, dtype=jnp.int32)
    length = jnp.sum(jnp.where(request_ids == request, lengths, 0))
    grouped = parents.reshape(steps, BEAMS, stride)
    parent_table = jnp.sum(jnp.where(request_ids[None, None, :] == request, grouped, 0), axis=2)
    slots = jnp.arange(cache_len, dtype=jnp.int32)
    beam_ids = jnp.arange(BEAMS, dtype=jnp.int32)
    mem_keys = memory[0, 0].astype(jnp.float32).reshape(-1, local_heads, HD)
    mem_values = memory[0, 1].astype(jnp.float32).reshape(-1, local_heads, HD)
    cross_valid = jnp.ones((BEAMS, mem_keys.shape[0]), dtype=bool)
    init_rows = init_cache[0]
    cache = init_rows
    proj_weight = out_weight.reshape(2 * width_local, out_weight.shape[2])
    own_query = queries[0, 0]
    parent_beam = jnp.sum(jnp.where(beam_ids == own_beam, parent_table[0], 0))
    cache = take_from(cache, parent_beam, own_beam, stride)
    cache = jnp.where((slots == length + 0)[None, :, None], new_kv[0, 0][:, None, :], cache)
    self_query = own_query[0].astype(jnp.float32).reshape(1, local_heads, HD)
    keys = cache[0].astype(jnp.float32).reshape(cache_len, local_heads, HD)
    values = cache[1].astype(jnp.float32).reshape(cache_len, local_heads, HD)
    valid = (slots <= length + 0)[None, :]
    weighted, peak, total = attend(self_query, keys, values, valid)
    self_out = (weighted / total[..., None])[0]
    items = spread(own_query[1], stride)
    cross_query = items.astype(jnp.float32).reshape(BEAMS, local_heads, HD)
    weighted, peak, total = attend(cross_query, mem_keys, mem_values, cross_valid)
    merged = combine(collect(weighted[:, None], peak[:, None], total[:, None], stride))
    cross_out = merged[0]
    attended = jnp.stack([self_out, cross_out]).reshape(1, 2 * width_local).astype(jnp.bfloat16)
    partial_proj = jnp.dot(
        lax.all_gather(attended, "batch", axis=0, tiled=True),
        proj_weight,
        preferred_element_type=jnp.float32,
    )
    projected = lax.psum(partial_proj, "tensor")
    hidden = (residual[0].astype(jnp.float32) + projected).astype(jnp.bfloat16)
    pre_act = jnp.dot(
        lax.all_gather(hidden, "batch", axis=1, tiled=True),
        up_weight,
        preferred_element_type=jnp.float32,
    )
    activation = jax.nn.gelu(pre_act, approximate=False).astype(jnp.bfloat16)
    joined = lax.all_gather(activation, "tensor", axis=1, tiled=True)
    ffn_row = lax.psum_scatter(
        jnp.dot(joined, down_weight, preferred_element_type=jnp.float32),
        "batch",
        scatter_dimension=0,
        tiled=True,
    ).astype(jnp.bfloat16)
    hidden_list = [hidden]
    ffn_list = [ffn_row]
    return (jnp.stack(hidden_list), jnp.stack(ffn_list), cache[None])


LANES = 128
SLOTS = 16
PIECES = 8
INWARD = (2, 1, 3, 2, 0, 0, 0)
ACROSS = (0, 1, 2, 3, 2, 0, 0)
OUTWARD = (0, 0, 1, 2, 3, 1, 1)
F32 = jnp.float32
BF16 = jnp.bfloat16


def step_kernel(
    q_hbm,
    kv_hbm,
    cache_hbm,
    mem_hbm,
    res_hbm,
    ow_hbm,
    up_hbm,
    dn_hbm,
    par_hbm,
    len_hbm,
    hid_out,
    ffn_out,
    cache_out,
    qall,
    kv,
    rows,
    mem,
    res,
    ow,
    up,
    dn,
    part_s,
    part_r,
    att,
    lhs,
    pp_s,
    pp_r,
    hid_all,
    acc,
    act,
    dacc,
    rs_s,
    rs_r,
    row_s,
    row_r,
    local_sem,
    q_send,
    q_recv,
    part_send,
    part_recv,
    att_send,
    att_recv,
    pair_send,
    pair_recv,
    hid_send,
    hid_recv,
    rs_send,
    rs_recv,
    near_send,
    far_send,
    row_recv,
    x_send,
    x_recv,
    out_send,
    out_recv,
    par_ref,
    len_ref,
):
    me = lax.axis_index("batch")
    half = lax.axis_index("tensor")
    other = 1 - half
    z, x = me // 2, me % 2
    heads = qall.shape[2] // LANES
    width = qall.shape[2]
    cache_len = rows.shape[2]
    block = hid_all.shape[2]
    chunks = rs_s.shape[0]
    zs = BEAMS // 2
    flip = z // 2
    turn = 1 - 2 * flip
    inner = z * turn + 3 * flip

    def nearest(j):
        k = j // 2 - 1
        there = (k + (k + 4 - inner) // 4) * turn + 3 * flip
        return there * 2 + (x + j) % 2

    sources = [me + 1 - 2 * x] + [nearest(j) for j in range(2, BEAMS)]
    peers = sources[::-1]

    def remote(src, dst, send, recv, device):
        return pltpu.make_async_remote_copy(
            src_ref=src,
            dst_ref=dst,
            send_sem=send,
            recv_sem=recv,
            device_id=device,
            device_id_type=pl.DeviceIdType.MESH,
        )

    locals_ = [
        pltpu.make_async_copy(q_hbm.at[0, 0], qall.at[me], local_sem.at[0]),
        pltpu.make_async_copy(kv_hbm.at[0, 0], kv, local_sem.at[1]),
        pltpu.make_async_copy(cache_hbm.at[0], rows.at[z], local_sem.at[2]),
        pltpu.make_async_copy(mem_hbm.at[0], mem, local_sem.at[3]),
        pltpu.make_async_copy(res_hbm.at[0], res, local_sem.at[4]),
        pltpu.make_async_copy(ow_hbm, ow, local_sem.at[5]),
        pltpu.make_async_copy(up_hbm, up, local_sem.at[6]),
        pltpu.make_async_copy(dn_hbm, dn, local_sem.at[7]),
        pltpu.make_async_copy(par_hbm, par_ref, local_sem.at[8]),
        pltpu.make_async_copy(len_hbm, len_ref, local_sem.at[9]),
    ]
    barrier = pltpu.get_barrier_semaphore()
    for peer in peers:
        pl.semaphore_signal(
            barrier, inc=1, device_id={"batch": peer}, device_id_type=pl.DeviceIdType.MESH
        )
    pl.semaphore_signal(
        barrier, inc=1, device_id={"tensor": other}, device_id_type=pl.DeviceIdType.MESH
    )
    for copy in locals_[:2] + locals_[8:] + locals_[2:8]:
        copy.start()
    part_s[...] = jnp.zeros_like(part_s)
    locals_[0].wait()
    pl.semaphore_wait(barrier, BEAMS)

    def to_peers(buffer_of, target_of, send, recv):
        sent = []
        for peer in peers:
            copy = remote(
                buffer_of(peer), target_of(me), send.at[peer], recv.at[me], {"batch": peer}
            )
            copy.start()
            sent.append(copy)
        return sent

    def arrived(target_of, recv, source):
        remote(
            target_of(source), target_of(source), recv.at[source], recv.at[source],
            {"batch": source},
        ).wait_recv()

    sent = to_peers(lambda p: qall.at[me], lambda s: qall.at[s], q_send, q_recv)

    pieces = row_recv.shape[1]
    span = cache_len * 2 // pieces
    partner = me + 1 - 2 * x
    ahead = (me + BEAMS + 2 * turn) % BEAMS
    beyond = (me + BEAMS + 4 * turn) % BEAMS
    outer = (me + BEAMS - 2 * turn) % BEAMS
    beside = (partner + BEAMS - 2 * turn) % BEAMS
    is_end, is_mid = inner == 0, inner == 1

    def piece_of(ref, k):
        return ref.at[k * span // cache_len, pl.ds(k * span % cache_len, span)]

    def inward(k, send, to, slot):
        view = piece_of(rows.at[slot], k)
        return remote(view, view, send.at[k], row_recv.at[slot, k], {"batch": to})

    def across(j, k):
        return remote(
            piece_of(row_s.at[j], k), piece_of(row_r.at[j], k), x_send.at[j, k], x_recv.at[j, k],
            {"batch": partner},
        )

    def outward(k):
        return remote(
            piece_of(row_s.at[2], k), piece_of(row_r.at[2], k), out_send.at[k], out_recv.at[k],
            {"batch": outer},
        )

    def row_of(beam, which, at):
        wanted = par_ref[0, beam] // 2
        chosen = rows[0, which, at : at + span]
        for index in range(1, zs):
            chosen = jnp.where(wanted == index, rows[index, which, at : at + span], chosen)
        return chosen

    def start_inward(k):
        inward(k, near_send, ahead, z).start()

        @pl.when(is_end)
        def _():
            inward(k, far_send, beyond, z).start()

    def start_across(k):
        which, at = k * span // cache_len, k * span % cache_len

        @pl.when(is_mid)
        def _():
            for slot in (z - turn, z + turn, z + 2 * turn):
                slot = (slot + zs) % zs
                inward(k, near_send, ahead, slot).wait_recv()
            for j, beam in enumerate((partner, beside)):
                row_s[j, which, at : at + span] = row_of(beam, which, at)
                across(j, k).start()

    def start_outward(k):
        which, at = k * span // cache_len, k * span % cache_len

        @pl.when(is_mid)
        def _():
            across(1, k).wait_recv()
            row_s[2, which, at : at + span] = jnp.where(
                par_ref[0, outer] % 2 == x, row_of(outer, which, at),
                row_r[1, which, at : at + span],
            )
            outward(k).start()

    def rows_sent():
        for k in range(pieces):
            inward(k, near_send, ahead, z).wait_send()

            @pl.when(is_end)
            def _():
                inward(k, far_send, beyond, z).wait_send()

            @pl.when(is_mid)
            def _():
                across(0, k).wait_send()
                across(1, k).wait_send()
                outward(k).wait_send()

    def bulk(stage):
        for counts, start in ((INWARD, start_inward), (ACROSS, start_across), (OUTWARD, start_outward)):
            for k in range(sum(counts[:stage]), sum(counts[: stage + 1])):
                start(k)

    def finish_rows():
        time = lax.broadcasted_iota(jnp.int32, (span, width), 0)
        for k in range(pieces):
            which, at = k * span // cache_len, k * span % cache_len
            fresh = jnp.broadcast_to(new_f[which : which + 1], (span, width))

            def put(kept):
                cache_out[0, which, at : at + span] = jnp.where(
                    time + at == length, fresh, kept.astype(F32)
                ).astype(BF16)

            @pl.when(is_mid)
            def _():
                across(0, k).wait_recv()
                put(jnp.where(
                    parent % 2 == x, row_of(me, which, at), row_r[0, which, at : at + span]
                ))

            @pl.when(is_end)
            def _():
                outward(k).wait_recv()
                put(row_r[2, which, at : at + span])

    locals_[8].wait()
    locals_[9].wait()
    locals_[2].wait()
    bulk(0)
    locals_[1].wait()
    locals_[3].wait()
    for source in sources:
        arrived(lambda s: qall.at[s], q_recv, source)

    length = len_ref[0]
    queries = qall[...].astype(F32)
    lane = lax.broadcasted_iota(jnp.int32, (BEAMS, LANES), 1)
    stats = jnp.zeros((BEAMS, LANES), F32)
    slot = lax.broadcasted_iota(jnp.int32, (heads * BEAMS, cache_len), 1)
    for kind in range(2):
        def block_of(which, h):
            cut = slice(h * LANES, (h + 1) * LANES)
            return mem[which, :, cut] if kind else rows[z, which, :, cut]

        scores = jnp.concatenate(
            [
                lax.dot_general(
                    queries[:, kind, h * LANES : (h + 1) * LANES].astype(BF16),
                    block_of(0, h),
                    (((1,), (1,)), ((), ())),
                    preferred_element_type=F32,
                )
                for h in range(heads)
            ],
            axis=0,
        ) / math.sqrt(HD)
        if kind == 0:
            scores = jnp.where(slot < length, scores, -1e30)
        peak = jnp.max(scores, axis=1, keepdims=True)
        weights = jnp.exp(scores - peak)
        if kind == 0:
            weights = jnp.where(slot < length, weights, 0.0)
        total = jnp.sum(weights, axis=1, keepdims=True)
        for h in range(heads):
            cut = slice(h * BEAMS, (h + 1) * BEAMS)
            w = weights[cut]
            high = w.astype(BF16)
            low = (w - high.astype(F32)).astype(BF16)
            both = jnp.dot(
                jnp.concatenate([high, low], axis=0),
                block_of(1, h),
                preferred_element_type=F32,
            )
            part_s[:, kind * SLOTS + h, :] = both[:BEAMS] + both[BEAMS:]
            stats = jnp.where(lane == 2 * kind * SLOTS + h, peak[cut], stats)
            stats = jnp.where(lane == (2 * kind + 1) * SLOTS + h, total[cut], stats)
    part_s[:, heads, :] = stats
    sent += to_peers(lambda p: part_s.at[p], lambda s: part_r.at[s], part_send, part_recv)
    bulk(1)
    part_r[me] = part_s[me]

    def rows_of(flat):
        return jnp.concatenate(
            [flat[:, h * LANES : (h + 1) * LANES] for h in range(heads)], axis=0
        )

    own_q = qall[me].astype(F32)
    new_f = kv[...].astype(F32)
    new_score = jnp.sum(rows_of(own_q[0:1] * new_f[0:1]), axis=1, keepdims=True) / math.sqrt(HD)
    new_value = rows_of(new_f[1:2])
    for source in sources:
        arrived(lambda s: part_r.at[s], part_recv, source)
    parent = par_ref[0, me]
    turned = part_r[:, heads, :].T
    beam = lax.broadcasted_iota(jnp.int32, (LANES, BEAMS), 1)
    chosen = jnp.sum(jnp.where(beam == parent, turned, 0.0), axis=1, keepdims=True)
    self_peak, self_total = chosen[:heads], chosen[SLOTS : SLOTS + heads]
    self_part = part_r[parent][:heads]
    top = jnp.maximum(self_peak, new_score)
    old_f, new_w = jnp.exp(self_peak - top), jnp.exp(new_score - top)
    self_out = (old_f * self_part + new_w * new_value) / (old_f * self_total + new_w)
    peaks = turned[2 * SLOTS : 2 * SLOTS + heads]
    factor = jnp.exp(peaks - jnp.max(peaks, axis=1, keepdims=True))
    denom = jnp.sum(factor * turned[3 * SLOTS : 3 * SLOTS + heads], axis=1, keepdims=True)
    numer = jnp.zeros((heads, LANES), F32)
    for p in range(BEAMS):
        numer = numer + factor[:, p : p + 1] * part_r[p][SLOTS : SLOTS + heads]
    cross_out = numer / denom
    spare = jnp.zeros((SLOTS - heads, LANES), F32)
    att[me] = jnp.concatenate([self_out, spare, cross_out, spare], axis=0).astype(BF16)
    sent += to_peers(lambda p: att.at[me], lambda s: att.at[s], att_send, att_recv)
    bulk(2)
    locals_[4].wait()
    locals_[5].wait()
    for source in sources:
        arrived(lambda s: att.at[s], att_recv, source)
    attended = att[...].astype(F32)
    for kind in range(2):
        for h in range(heads):
            lhs[kind, :, h * LANES : (h + 1) * LANES] = attended[:, kind * SLOTS + h, :].astype(BF16)
    pp_s[...] = jnp.dot(lhs[0], ow[0], preferred_element_type=F32) + jnp.dot(
        lhs[1], ow[1], preferred_element_type=F32
    )
    pair = remote(pp_s, pp_r, pair_send.at[0], pair_recv.at[0], {"tensor": other})
    pair.start()
    pair.wait_recv()
    hidden = (res[...].astype(F32) + (pp_s[...] + pp_r[...])).astype(BF16)
    hid_all[me] = hidden
    sent += [pair] + to_peers(
        lambda p: hid_all.at[me], lambda s: hid_all.at[s], hid_send, hid_recv
    )
    hid_out[0] = hidden
    bulk(3)
    locals_[6].wait()

    def up_dot(source):
        at = pl.multiple_of(source * block, block)
        return jnp.dot(hid_all[source], up[pl.ds(at, block), :], preferred_element_type=F32)

    acc[...] = up_dot(me)
    arrived(lambda s: hid_all.at[s], hid_recv, sources[0])
    acc[...] += up_dot(sources[0])

    def up_step(j, carry):
        source = nearest(j)
        arrived(lambda s: hid_all.at[s], hid_recv, source)
        acc[...] += up_dot(source)
        return carry

    lax.fori_loop(2, BEAMS, up_step, 0)
    pre = acc[...]
    act[half] = (0.5 * pre * (1.0 + lax.erf(pre * math.sqrt(0.5)))).astype(BF16)
    swap = remote(act.at[half], act.at[half], pair_send.at[1], pair_recv.at[1], {"tensor": other})
    swap.start()
    sent.append(swap)
    bulk(4)
    locals_[7].wait()
    part = rs_s.shape[2] * LANES

    def down_dot(which, c):
        at = pl.multiple_of(which * width, width)
        return jnp.dot(
            act[which],
            dn[pl.ds(at, width), pl.ds(pl.multiple_of(c * part, part), part)],
            preferred_element_type=F32,
        )

    def own_half(c, carry):
        dacc[c] = down_dot(half, c)
        return carry

    lax.fori_loop(0, chunks, own_half, 0)
    bulk(5)
    swap.wait_recv()

    def other_half(c, carry):
        sums = dacc[c] + down_dot(other, c)
        for i in range(part // LANES):
            rs_s[c, :, i, :] = sums[:, i * LANES : (i + 1) * LANES]
        for peer in peers:
            remote(
                rs_s.at[c, peer], rs_r.at[c, me], rs_send.at[c, peer], rs_recv.at[c, me],
                {"batch": peer},
            ).start()
        rs_r[c, me] = rs_s[c, me]
        return carry

    lax.fori_loop(0, chunks, other_half, 0)
    bulk(6)
    finish_rows()
    for copy in sent:
        copy.wait_send()
    rows_sent()

    def collect_chunk(c):
        for source in sources:
            remote(
                rs_r.at[c, source], rs_r.at[c, source], rs_recv.at[c, source],
                rs_recv.at[c, source], {"batch": source},
            ).wait_recv()
        sums = rs_r[c, 0]
        for p in range(1, BEAMS):
            sums = sums + rs_r[c, p]
        for i in range(part // LANES):
            at = c * part + i * LANES
            ffn_out[0, 0:1, at : at + LANES] = sums[i : i + 1].astype(BF16)

    for c in range(chunks):
        collect_chunk(c)
    for c in range(chunks):
        for peer in peers:
            remote(
                rs_s.at[c, peer], rs_r.at[c, me], rs_send.at[c, peer], rs_recv.at[c, me],
                {"batch": peer},
            ).wait_send()


def place_kernel(*refs):
    count = (len(refs) - 1) // 2
    sem = refs[-1]
    copies = [
        pltpu.make_async_copy(refs[i], refs[count + i], sem.at[i]) for i in range(count)
    ]
    for copy in copies:
        copy.start()
    for copy in copies:
        copy.wait()


def place(*arrays):
    any_ = pl.BlockSpec(memory_space=pl.ANY)
    vmem = pl.BlockSpec(memory_space=pltpu.VMEM)
    count = len(arrays)
    return pl.pallas_call(
        place_kernel,
        out_shape=tuple(jax.ShapeDtypeStruct(a.shape, a.dtype) for a in arrays),
        in_specs=[vmem] * count,
        out_specs=(any_,) * count,
        scratch_shapes=[pltpu.SemaphoreType.DMA((count,))],
    )(*(pltpu.with_memory_space_constraint(a, pltpu.VMEM) for a in arrays))


def kernel_body(
    init_cache,
    memory,
    queries,
    new_kv,
    residual,
    out_weight,
    up_weight,
    down_weight,
    parents,
    lengths,
):
    width = queries.shape[-1]
    row = init_cache.shape[1:]
    block = residual.shape[-1]
    columns = down_weight.shape[1]
    chunks = 3 if columns % (3 * 8 * LANES) == 0 else 1
    part_rows = columns // chunks // LANES
    any_ = pl.BlockSpec(memory_space=pl.ANY)
    vmem = pl.BlockSpec(memory_space=pltpu.VMEM)
    hbm = pl.BlockSpec(memory_space=pltpu.HBM)
    dma = pltpu.SemaphoreType.DMA
    results = pl.pallas_call(
        step_kernel,
        out_shape=(
            pltpu.VMEM(residual.shape, BF16),
            pltpu.VMEM((1, 1, columns), BF16),
            pltpu.VMEM(init_cache.shape, BF16),
        ),
        in_specs=[any_] * 8 + [hbm] * 2,
        out_specs=(vmem, vmem, vmem),
        scratch_shapes=[
            pltpu.VMEM((BEAMS, 2, width), BF16),
            pltpu.VMEM((2, width), BF16),
            pltpu.VMEM((BEAMS // 2,) + row, BF16),
            pltpu.VMEM(row, BF16),
            pltpu.VMEM((BEAMS, block), BF16),
            pltpu.VMEM(out_weight.shape, BF16),
            pltpu.VMEM(up_weight.shape, BF16),
            pltpu.VMEM(down_weight.shape, BF16),
            pltpu.VMEM((BEAMS, 2 * SLOTS, LANES), F32),
            pltpu.VMEM((BEAMS, 2 * SLOTS, LANES), F32),
            pltpu.VMEM((BEAMS, 2 * SLOTS, LANES), BF16),
            pltpu.VMEM((2, BEAMS, width), BF16),
            pltpu.VMEM((BEAMS, block), F32),
            pltpu.VMEM((BEAMS, block), F32),
            pltpu.VMEM((BEAMS, BEAMS, block), BF16),
            pltpu.VMEM((BEAMS, up_weight.shape[1]), F32),
            pltpu.VMEM((2, BEAMS, up_weight.shape[1]), BF16),
            pltpu.VMEM((chunks, BEAMS, columns // chunks), F32),
            pltpu.VMEM((chunks, BEAMS, part_rows, LANES), F32),
            pltpu.VMEM((chunks, BEAMS, part_rows, LANES), F32),
            pltpu.VMEM((3,) + row, BF16),
            pltpu.VMEM((3,) + row, BF16),
            dma((10,)),
            dma((BEAMS,)),
            dma((BEAMS,)),
            dma((BEAMS,)),
            dma((BEAMS,)),
            dma((BEAMS,)),
            dma((BEAMS,)),
            dma((2,)),
            dma((2,)),
            dma((BEAMS,)),
            dma((BEAMS,)),
            dma((chunks, BEAMS)),
            dma((chunks, BEAMS)),
            dma((PIECES,)),
            dma((PIECES,)),
            dma((BEAMS // 2, PIECES)),
            dma((2, PIECES)),
            dma((2, PIECES)),
            dma((PIECES,)),
            dma((PIECES,)),
            pltpu.SMEM(parents.shape, jnp.int32),
            pltpu.SMEM(lengths.shape, jnp.int32),
        ],
        compiler_params=pltpu.CompilerParams(
            collective_id=0, has_side_effects=True, vmem_limit_bytes=62 * 1024 * 1024
        ),
    )(
        queries,
        new_kv,
        init_cache,
        memory,
        residual,
        out_weight,
        up_weight,
        down_weight,
        parents,
        lengths,
    )
    return place(*results)


def solution(mesh):
    placed = (
        P(("grp", "batch"), None, None, "tensor"),
        P(("grp", "batch"), None, None, "tensor"),
        P(None, ("grp", "batch"), None, "tensor"),
        P(None, ("grp", "batch"), None, "tensor"),
        P(None, "grp", "batch"),
        P(None, "tensor", "batch"),
        P(None, ("batch", "tensor")),
        P("batch", "tensor"),
        P(None, "grp"),
        P("grp"),
    )
    one_request = mesh.shape["batch"] == BEAMS and mesh.shape["tensor"] == 2
    return jax.shard_map(
        kernel_body if one_request else body,
        mesh=mesh,
        in_specs=placed,
        out_specs=(
            P(None, "grp", "batch"),
            P(None, ("grp", "batch"), "tensor"),
            P(("grp", "batch"), None, None, "tensor"),
        ),
        check_vma=False,
    )
```

```python
import math

import jax
import jax.numpy as jnp
from jax import lax
from jax.experimental import pallas as pl
from jax.experimental.pallas import tpu as pltpu
from jax.sharding import PartitionSpec as P

HD = 128
BEAMS = 8


def from_behind(value, axis, by):
    devices = lax.axis_size(axis)
    return lax.ppermute(value, axis, [(i, (i + by) % devices) for i in range(devices)])


def attend(query, keys, values, valid):
    highest = lax.Precision.HIGHEST
    scores = jnp.einsum("nhd,chd->nhc", query, keys, precision=highest) / math.sqrt(HD)
    mask = valid[:, None, :]
    masked = jnp.where(mask, scores, -1e30)
    peak = jnp.max(masked, axis=-1)
    weights = jnp.where(mask, jnp.exp(masked - peak[..., None]), 0.0)
    total = jnp.sum(weights, axis=-1)
    weighted = jnp.einsum("nhc,chd->nhd", weights, values, precision=highest)
    return (weighted, peak, total)


def spread(payload, stride):
    items = [payload]
    for offset in range(1, BEAMS):
        items.append(from_behind(payload, "batch", offset * stride))
    return jnp.stack(items)


def take_from(block, source, own_beam, stride):
    wanted = (own_beam - source) % BEAMS
    result = block
    for offset in range(1, BEAMS):
        moved = from_behind(block, "batch", offset * stride)
        result = jnp.where(wanted == offset, moved, result)
    return result


def collect(weighted, peak, total, stride):
    gathered = [(weighted[0], peak[0], total[0])]
    for offset in range(1, BEAMS):
        gathered.append(
            from_behind((weighted[offset], peak[offset], total[offset]), "batch", -offset * stride)
        )
    return gathered


def combine(gathered):
    peaks = jnp.stack([entry[1] for entry in gathered])
    top = jnp.max(peaks, axis=0)
    factors = jnp.exp(peaks - top[None])
    numer = jnp.sum(jnp.stack([entry[0] for entry in gathered]) * factors[..., None], axis=0)
    denom = jnp.sum(jnp.stack([entry[2] for entry in gathered]) * factors, axis=0)
    return numer / denom[..., None]


def body(
    init_cache,
    memory,
    queries,
    new_kv,
    residual,
    out_weight,
    up_weight,
    down_weight,
    parents,
    lengths,
):
    stride = lax.axis_size("batch") // BEAMS
    position = lax.axis_index("batch")
    own_beam = position // stride
    request = position % stride
    width_local = queries.shape[-1]
    local_heads = width_local // HD
    cache_len = init_cache.shape[2]
    steps = queries.shape[0]
    request_ids = jnp.arange(stride, dtype=jnp.int32)
    length = jnp.sum(jnp.where(request_ids == request, lengths, 0))
    grouped = parents.reshape(steps, BEAMS, stride)
    parent_table = jnp.sum(jnp.where(request_ids[None, None, :] == request, grouped, 0), axis=2)
    slots = jnp.arange(cache_len, dtype=jnp.int32)
    beam_ids = jnp.arange(BEAMS, dtype=jnp.int32)
    mem_keys = memory[0, 0].astype(jnp.float32).reshape(-1, local_heads, HD)
    mem_values = memory[0, 1].astype(jnp.float32).reshape(-1, local_heads, HD)
    cross_valid = jnp.ones((BEAMS, mem_keys.shape[0]), dtype=bool)
    init_rows = init_cache[0]
    cache = init_rows
    proj_weight = out_weight.reshape(2 * width_local, out_weight.shape[2])
    own_query = queries[0, 0]
    parent_beam = jnp.sum(jnp.where(beam_ids == own_beam, parent_table[0], 0))
    cache = take_from(cache, parent_beam, own_beam, stride)
    cache = jnp.where((slots == length + 0)[None, :, None], new_kv[0, 0][:, None, :], cache)
    self_query = own_query[0].astype(jnp.float32).reshape(1, local_heads, HD)
    keys = cache[0].astype(jnp.float32).reshape(cache_len, local_heads, HD)
    values = cache[1].astype(jnp.float32).reshape(cache_len, local_heads, HD)
    valid = (slots <= length + 0)[None, :]
    weighted, peak, total = attend(self_query, keys, values, valid)
    self_out = (weighted / total[..., None])[0]
    items = spread(own_query[1], stride)
    cross_query = items.astype(jnp.float32).reshape(BEAMS, local_heads, HD)
    weighted, peak, total = attend(cross_query, mem_keys, mem_values, cross_valid)
    merged = combine(collect(weighted[:, None], peak[:, None], total[:, None], stride))
    cross_out = merged[0]
    attended = jnp.stack([self_out, cross_out]).reshape(1, 2 * width_local).astype(jnp.bfloat16)
    partial_proj = jnp.dot(
        lax.all_gather(attended, "batch", axis=0, tiled=True),
        proj_weight,
        preferred_element_type=jnp.float32,
    )
    projected = lax.psum(partial_proj, "tensor")
    hidden = (residual[0].astype(jnp.float32) + projected).astype(jnp.bfloat16)
    pre_act = jnp.dot(
        lax.all_gather(hidden, "batch", axis=1, tiled=True),
        up_weight,
        preferred_element_type=jnp.float32,
    )
    activation = jax.nn.gelu(pre_act, approximate=False).astype(jnp.bfloat16)
    joined = lax.all_gather(activation, "tensor", axis=1, tiled=True)
    ffn_row = lax.psum_scatter(
        jnp.dot(joined, down_weight, preferred_element_type=jnp.float32),
        "batch",
        scatter_dimension=0,
        tiled=True,
    ).astype(jnp.bfloat16)
    hidden_list = [hidden]
    ffn_list = [ffn_row]
    return (jnp.stack(hidden_list), jnp.stack(ffn_list), cache[None])


LANES = 128
SLOTS = 16
PIECES = 8
INWARD = (2, 1, 3, 2, 0, 0, 0)
ACROSS = (0, 1, 2, 3, 2, 0, 0)
OUTWARD = (0, 0, 1, 2, 3, 1, 1)
F32 = jnp.float32
BF16 = jnp.bfloat16


def step_kernel(
    q_hbm,
    kv_hbm,
    cache_hbm,
    mem_hbm,
    res_hbm,
    ow_hbm,
    up_hbm,
    dn_hbm,
    par_hbm,
    len_hbm,
    hid_out,
    ffn_out,
    cache_out,
    qall,
    kv,
    rows,
    mem,
    res,
    ow,
    up,
    dn,
    part_s,
    part_r,
    att,
    lhs,
    pp_s,
    pp_r,
    hid_all,
    acc,
    act,
    dacc,
    rs_s,
    rs_r,
    row_s,
    row_r,
    local_sem,
    q_send,
    q_recv,
    part_send,
    part_recv,
    att_send,
    att_recv,
    pair_send,
    pair_recv,
    hid_send,
    hid_recv,
    rs_send,
    rs_recv,
    near_send,
    far_send,
    row_recv,
    x_send,
    x_recv,
    out_send,
    out_recv,
    par_ref,
    len_ref,
):
    me = lax.axis_index("batch")
    half = lax.axis_index("tensor")
    other = 1 - half
    z, x = me // 2, me % 2
    heads = qall.shape[2] // LANES
    width = qall.shape[2]
    cache_len = rows.shape[2]
    block = hid_all.shape[2]
    chunks = rs_s.shape[0]
    zs = BEAMS // 2
    flip = z // 2
    turn = 1 - 2 * flip
    inner = z * turn + 3 * flip

    def nearest(j):
        k = j // 2 - 1
        there = (k + (k + 4 - inner) // 4) * turn + 3 * flip
        return there * 2 + (x + j) % 2

    partner = me + 1 - 2 * x
    sources = [partner] + [nearest(j) for j in range(2, BEAMS)]
    peers = sources[::-1]

    def remote(src, dst, send, recv, device):
        return pltpu.make_async_remote_copy(
            src_ref=src,
            dst_ref=dst,
            send_sem=send,
            recv_sem=recv,
            device_id=device,
            device_id_type=pl.DeviceIdType.MESH,
        )

    locals_ = [
        pltpu.make_async_copy(q_hbm.at[0, 0], qall.at[me], local_sem.at[0]),
        pltpu.make_async_copy(kv_hbm.at[0, 0], kv, local_sem.at[1]),
        pltpu.make_async_copy(cache_hbm.at[0], rows.at[z], local_sem.at[2]),
        pltpu.make_async_copy(mem_hbm.at[0], mem, local_sem.at[3]),
        pltpu.make_async_copy(res_hbm.at[0], res, local_sem.at[4]),
        pltpu.make_async_copy(ow_hbm, ow, local_sem.at[5]),
        pltpu.make_async_copy(up_hbm, up, local_sem.at[6]),
        pltpu.make_async_copy(dn_hbm, dn, local_sem.at[7]),
        pltpu.make_async_copy(par_hbm, par_ref, local_sem.at[8]),
        pltpu.make_async_copy(len_hbm, len_ref, local_sem.at[9]),
    ]
    barrier = pltpu.get_barrier_semaphore()
    for peer in peers:
        pl.semaphore_signal(
            barrier, inc=1, device_id={"batch": peer}, device_id_type=pl.DeviceIdType.MESH
        )
    pl.semaphore_signal(
        barrier, inc=1, device_id={"tensor": other}, device_id_type=pl.DeviceIdType.MESH
    )
    for copy in locals_[:2] + locals_[8:] + locals_[2:8]:
        copy.start()
    part_s[...] = jnp.zeros_like(part_s)
    locals_[0].wait()
    pl.semaphore_wait(barrier, BEAMS)

    def to_peers(buffer_of, target_of, send, recv):
        for peer in peers:
            remote(buffer_of(peer), target_of(me), send, recv, {"batch": peer}).start()
        return [all_of(target_of, send)]

    def all_of(target_of, sem):
        view = target_of(pl.ds(0, BEAMS - 1))
        return remote(view, view, sem, sem, {"batch": partner})

    def arrived(target_of, recv, source):
        remote(
            target_of(source), target_of(source), recv.at[source], recv.at[source],
            {"batch": source},
        ).wait_recv()

    sent = to_peers(lambda p: qall.at[me], lambda s: qall.at[s], q_send.at[0], q_recv.at[0])

    pieces = row_recv.shape[0]
    span = cache_len * 2 // pieces
    ahead = (me + BEAMS + 2 * turn) % BEAMS
    beyond = (me + BEAMS + 4 * turn) % BEAMS
    outer = (me + BEAMS - 2 * turn) % BEAMS
    beside = (partner + BEAMS - 2 * turn) % BEAMS
    is_end, is_mid = inner == 0, inner == 1

    def piece_of(ref, k):
        return ref.at[k * span // cache_len, pl.ds(k * span % cache_len, span)]

    def inward(k, send, to, slot):
        view = piece_of(rows.at[slot], k)
        return remote(view, view, send, row_recv.at[k], {"batch": to})

    def across(j, k):
        return remote(
            piece_of(row_s.at[j], k), piece_of(row_r.at[j], k), x_send.at[0],
            x_recv.at[j * (2 + k) + (1 - j) * (2 * k // pieces)], {"batch": partner},
        )

    def outward(k):
        return remote(
            piece_of(row_s.at[2], k), piece_of(row_r.at[2], k), out_send.at[0],
            out_recv.at[2 * k // pieces],
            {"batch": outer},
        )

    def row_of(beam, which, at):
        wanted = par_ref[0, beam] // 2
        chosen = rows[0, which, at : at + span]
        for index in range(1, zs):
            chosen = jnp.where(wanted == index, rows[index, which, at : at + span], chosen)
        return chosen

    def start_inward(k):
        inward(k, near_send.at[0], ahead, z).start()

        @pl.when(is_end)
        def _():
            inward(k, far_send.at[0], beyond, z).start()

    def start_across(k):
        which, at = k * span // cache_len, k * span % cache_len

        @pl.when(is_mid)
        def _():
            three = rows.at[pl.ds(0, zs - 1), which, pl.ds(at, span)]
            remote(three, three, near_send.at[0], row_recv.at[k], {"batch": ahead}).wait_recv()
            for j, beam in enumerate((partner, beside)):
                row_s[j, which, at : at + span] = row_of(beam, which, at)
                across(j, k).start()

    def start_outward(k):
        which, at = k * span // cache_len, k * span % cache_len

        @pl.when(is_mid)
        def _():
            across(1, k).wait_recv()
            row_s[2, which, at : at + span] = jnp.where(
                par_ref[0, outer] % 2 == x, row_of(outer, which, at),
                row_r[1, which, at : at + span],
            )
            outward(k).start()

    def whole(view, sem, to):
        return remote(view, view, sem.at[0], sem.at[0], {"batch": to})

    def rows_sent():
        whole(rows.at[z], near_send, ahead).wait_send()

        @pl.when(is_end)
        def _():
            whole(rows.at[z], far_send, beyond).wait_send()

        @pl.when(is_mid)
        def _():
            whole(row_s.at[pl.ds(0, 2)], x_send, partner).wait_send()
            whole(row_s.at[2], out_send, outer).wait_send()

    def bulk(stage):
        for counts, start in ((INWARD, start_inward), (ACROSS, start_across), (OUTWARD, start_outward)):
            for k in range(sum(counts[:stage]), sum(counts[: stage + 1])):
                start(k)

    def finish_rows():
        time = lax.broadcasted_iota(jnp.int32, (cache_len, width), 0)
        for which in range(2):
            fresh = jnp.broadcast_to(new_f[which : which + 1], (cache_len, width))

            def put(kept):
                cache_out[0, which] = jnp.where(
                    time == length, fresh, kept.astype(F32)
                ).astype(BF16)

            @pl.when(is_mid)
            def _():
                view = row_r.at[0, which]
                remote(
                    view, view, x_recv.at[which], x_recv.at[which], {"batch": partner}
                ).wait_recv()
                mine = rows[0, which]
                for index in range(1, zs):
                    mine = jnp.where(parent // 2 == index, rows[index, which], mine)
                put(jnp.where(parent % 2 == x, mine, row_r[0, which]))

            @pl.when(is_end)
            def _():
                view = row_r.at[2, which]
                remote(
                    view, view, out_recv.at[which], out_recv.at[which], {"batch": outer}
                ).wait_recv()
                put(row_r[2, which])

    locals_[8].wait()
    locals_[9].wait()
    locals_[2].wait()
    bulk(0)
    locals_[1].wait()
    locals_[3].wait()
    all_of(lambda s: qall.at[s], q_recv.at[0]).wait_recv()

    length = len_ref[0]
    queries = qall[...].astype(F32)
    lane = lax.broadcasted_iota(jnp.int32, (BEAMS, LANES), 1)
    stats = jnp.zeros((BEAMS, LANES), F32)
    slot = lax.broadcasted_iota(jnp.int32, (heads * BEAMS, cache_len), 1)
    for kind in range(2):
        def block_of(which, h):
            cut = slice(h * LANES, (h + 1) * LANES)
            return mem[which, :, cut] if kind else rows[z, which, :, cut]

        scores = jnp.concatenate(
            [
                lax.dot_general(
                    queries[:, kind, h * LANES : (h + 1) * LANES].astype(BF16),
                    block_of(0, h),
                    (((1,), (1,)), ((), ())),
                    preferred_element_type=F32,
                )
                for h in range(heads)
            ],
            axis=0,
        ) / math.sqrt(HD)
        if kind == 0:
            scores = jnp.where(slot < length, scores, -1e30)
        peak = jnp.max(scores, axis=1, keepdims=True)
        weights = jnp.exp(scores - peak)
        if kind == 0:
            weights = jnp.where(slot < length, weights, 0.0)
        total = jnp.sum(weights, axis=1, keepdims=True)
        for h in range(heads):
            cut = slice(h * BEAMS, (h + 1) * BEAMS)
            w = weights[cut]
            high = w.astype(BF16)
            low = (w - high.astype(F32)).astype(BF16)
            both = jnp.dot(
                jnp.concatenate([high, low], axis=0),
                block_of(1, h),
                preferred_element_type=F32,
            )
            part_s[:, kind * SLOTS + h, :] = both[:BEAMS] + both[BEAMS:]
            stats = jnp.where(lane == 2 * kind * SLOTS + h, peak[cut], stats)
            stats = jnp.where(lane == (2 * kind + 1) * SLOTS + h, total[cut], stats)
    part_s[:, heads, :] = stats
    sent += to_peers(lambda p: part_s.at[p], lambda s: part_r.at[s], part_send.at[0], part_recv.at[0])
    bulk(1)
    part_r[me] = part_s[me]

    def rows_of(flat):
        return jnp.concatenate(
            [flat[:, h * LANES : (h + 1) * LANES] for h in range(heads)], axis=0
        )

    own_q = qall[me].astype(F32)
    new_f = kv[...].astype(F32)
    new_score = jnp.sum(rows_of(own_q[0:1] * new_f[0:1]), axis=1, keepdims=True) / math.sqrt(HD)
    new_value = rows_of(new_f[1:2])
    all_of(lambda s: part_r.at[s], part_recv.at[0]).wait_recv()
    parent = par_ref[0, me]
    turned = part_r[:, heads, :].T
    beam = lax.broadcasted_iota(jnp.int32, (LANES, BEAMS), 1)
    chosen = jnp.sum(jnp.where(beam == parent, turned, 0.0), axis=1, keepdims=True)
    self_peak, self_total = chosen[:heads], chosen[SLOTS : SLOTS + heads]
    self_part = part_r[parent][:heads]
    top = jnp.maximum(self_peak, new_score)
    old_f, new_w = jnp.exp(self_peak - top), jnp.exp(new_score - top)
    self_out = (old_f * self_part + new_w * new_value) / (old_f * self_total + new_w)
    peaks = turned[2 * SLOTS : 2 * SLOTS + heads]
    factor = jnp.exp(peaks - jnp.max(peaks, axis=1, keepdims=True))
    denom = jnp.sum(factor * turned[3 * SLOTS : 3 * SLOTS + heads], axis=1, keepdims=True)
    numer = jnp.zeros((heads, LANES), F32)
    for p in range(BEAMS):
        numer = numer + factor[:, p : p + 1] * part_r[p][SLOTS : SLOTS + heads]
    cross_out = numer / denom
    spare = jnp.zeros((SLOTS - heads, LANES), F32)
    att[me] = jnp.concatenate([self_out, spare, cross_out, spare], axis=0).astype(BF16)
    sent += to_peers(lambda p: att.at[me], lambda s: att.at[s], att_send.at[0], att_recv.at[0])
    bulk(2)
    locals_[4].wait()
    locals_[5].wait()
    all_of(lambda s: att.at[s], att_recv.at[0]).wait_recv()
    attended = att[...].astype(F32)
    for kind in range(2):
        for h in range(heads):
            lhs[kind, :, h * LANES : (h + 1) * LANES] = attended[:, kind * SLOTS + h, :].astype(BF16)
    pp_s[...] = jnp.dot(lhs[0], ow[0], preferred_element_type=F32) + jnp.dot(
        lhs[1], ow[1], preferred_element_type=F32
    )
    pair = remote(pp_s, pp_r, pair_send.at[0], pair_recv.at[0], {"tensor": other})
    pair.start()
    pair.wait_recv()
    hidden = (res[...].astype(F32) + (pp_s[...] + pp_r[...])).astype(BF16)
    hid_all[me] = hidden
    sent += [pair] + to_peers(
        lambda p: hid_all.at[me], lambda s: hid_all.at[s], hid_send.at[0], hid_recv.at[me]
    )
    hid_out[0] = hidden
    bulk(3)
    locals_[6].wait()

    def up_dot(source):
        at = pl.multiple_of(source * block, block)
        return jnp.dot(hid_all[source], up[pl.ds(at, block), :], preferred_element_type=F32)

    acc[...] = up_dot(me)
    arrived(lambda s: hid_all.at[s], hid_recv, sources[0])
    acc[...] += up_dot(sources[0])

    def up_step(j, carry):
        source = nearest(j)
        arrived(lambda s: hid_all.at[s], hid_recv, source)
        acc[...] += up_dot(source)
        return carry

    lax.fori_loop(2, BEAMS, up_step, 0)
    pre = acc[...]
    act[half] = (0.5 * pre * (1.0 + lax.erf(pre * math.sqrt(0.5)))).astype(BF16)
    swap = remote(act.at[half], act.at[half], pair_send.at[1], pair_recv.at[1], {"tensor": other})
    swap.start()
    sent.append(swap)
    bulk(4)
    locals_[7].wait()
    part = rs_s.shape[2] * LANES

    def down_dot(which, c):
        at = pl.multiple_of(which * width, width)
        return jnp.dot(
            act[which],
            dn[pl.ds(at, width), pl.ds(pl.multiple_of(c * part, part), part)],
            preferred_element_type=F32,
        )

    def own_half(c, carry):
        dacc[c] = down_dot(half, c)
        return carry

    lax.fori_loop(0, chunks, own_half, 0)
    bulk(5)
    swap.wait_recv()

    def other_half(c, carry):
        sums = dacc[c] + down_dot(other, c)
        for i in range(part // LANES):
            rs_s[c, :, i, :] = sums[:, i * LANES : (i + 1) * LANES]
        for peer in peers:
            remote(
                rs_s.at[c, peer], rs_r.at[c, me], rs_send.at[0], rs_recv.at[c], {"batch": peer}
            ).start()
        rs_r[c, me] = rs_s[c, me]
        return carry

    lax.fori_loop(0, chunks, other_half, 0)
    bulk(6)
    finish_rows()
    for copy in sent:
        copy.wait_send()
    rows_sent()

    def collect_chunk(c):
        all_of(lambda s: rs_r.at[c, s], rs_recv.at[c]).wait_recv()
        sums = rs_r[c, 0]
        for p in range(1, BEAMS):
            sums = sums + rs_r[c, p]
        for i in range(part // LANES):
            at = c * part + i * LANES
            ffn_out[0, 0:1, at : at + LANES] = sums[i : i + 1].astype(BF16)

    for c in range(chunks):
        collect_chunk(c)
    every = rs_s.at[:, pl.ds(0, BEAMS - 1)]
    remote(every, every, rs_send.at[0], rs_send.at[0], {"batch": partner}).wait_send()


def place_kernel(*refs):
    count = (len(refs) - 1) // 2
    sem = refs[-1]
    copies = [
        pltpu.make_async_copy(refs[i], refs[count + i], sem.at[i]) for i in range(count)
    ]
    for copy in copies:
        copy.start()
    for copy in copies:
        copy.wait()


def place(*arrays):
    any_ = pl.BlockSpec(memory_space=pl.ANY)
    vmem = pl.BlockSpec(memory_space=pltpu.VMEM)
    count = len(arrays)
    return pl.pallas_call(
        place_kernel,
        out_shape=tuple(jax.ShapeDtypeStruct(a.shape, a.dtype) for a in arrays),
        in_specs=[vmem] * count,
        out_specs=(any_,) * count,
        scratch_shapes=[pltpu.SemaphoreType.DMA((count,))],
    )(*(pltpu.with_memory_space_constraint(a, pltpu.VMEM) for a in arrays))


def kernel_body(
    init_cache,
    memory,
    queries,
    new_kv,
    residual,
    out_weight,
    up_weight,
    down_weight,
    parents,
    lengths,
):
    width = queries.shape[-1]
    row = init_cache.shape[1:]
    block = residual.shape[-1]
    columns = down_weight.shape[1]
    chunks = 3 if columns % (3 * 8 * LANES) == 0 else 1
    part_rows = columns // chunks // LANES
    any_ = pl.BlockSpec(memory_space=pl.ANY)
    vmem = pl.BlockSpec(memory_space=pltpu.VMEM)
    hbm = pl.BlockSpec(memory_space=pltpu.HBM)
    dma = pltpu.SemaphoreType.DMA
    results = pl.pallas_call(
        step_kernel,
        out_shape=(
            pltpu.VMEM(residual.shape, BF16),
            pltpu.VMEM((1, 1, columns), BF16),
            pltpu.VMEM(init_cache.shape, BF16),
        ),
        in_specs=[any_] * 8 + [hbm] * 2,
        out_specs=(vmem, vmem, vmem),
        scratch_shapes=[
            pltpu.VMEM((BEAMS, 2, width), BF16),
            pltpu.VMEM((2, width), BF16),
            pltpu.VMEM((BEAMS // 2,) + row, BF16),
            pltpu.VMEM(row, BF16),
            pltpu.VMEM((BEAMS, block), BF16),
            pltpu.VMEM(out_weight.shape, BF16),
            pltpu.VMEM(up_weight.shape, BF16),
            pltpu.VMEM(down_weight.shape, BF16),
            pltpu.VMEM((BEAMS, 2 * SLOTS, LANES), F32),
            pltpu.VMEM((BEAMS, 2 * SLOTS, LANES), F32),
            pltpu.VMEM((BEAMS, 2 * SLOTS, LANES), BF16),
            pltpu.VMEM((2, BEAMS, width), BF16),
            pltpu.VMEM((BEAMS, block), F32),
            pltpu.VMEM((BEAMS, block), F32),
            pltpu.VMEM((BEAMS, BEAMS, block), BF16),
            pltpu.VMEM((BEAMS, up_weight.shape[1]), F32),
            pltpu.VMEM((2, BEAMS, up_weight.shape[1]), BF16),
            pltpu.VMEM((chunks, BEAMS, columns // chunks), F32),
            pltpu.VMEM((chunks, BEAMS, part_rows, LANES), F32),
            pltpu.VMEM((chunks, BEAMS, part_rows, LANES), F32),
            pltpu.VMEM((3,) + row, BF16),
            pltpu.VMEM((3,) + row, BF16),
            dma((10,)),
            dma((1,)),
            dma((1,)),
            dma((1,)),
            dma((1,)),
            dma((1,)),
            dma((1,)),
            dma((2,)),
            dma((2,)),
            dma((1,)),
            dma((BEAMS,)),
            dma((1,)),
            dma((chunks,)),
            dma((1,)),
            dma((1,)),
            dma((PIECES,)),
            dma((1,)),
            dma((2 + PIECES,)),
            dma((1,)),
            dma((2,)),
            pltpu.SMEM(parents.shape, jnp.int32),
            pltpu.SMEM(lengths.shape, jnp.int32),
        ],
        compiler_params=pltpu.CompilerParams(
            collective_id=0, has_side_effects=True, vmem_limit_bytes=62 * 1024 * 1024
        ),
    )(
        queries,
        new_kv,
        init_cache,
        memory,
        residual,
        out_weight,
        up_weight,
        down_weight,
        parents,
        lengths,
    )
    return place(*results)


def solution(mesh):
    placed = (
        P(("grp", "batch"), None, None, "tensor"),
        P(("grp", "batch"), None, None, "tensor"),
        P(None, ("grp", "batch"), None, "tensor"),
        P(None, ("grp", "batch"), None, "tensor"),
        P(None, "grp", "batch"),
        P(None, "tensor", "batch"),
        P(None, ("batch", "tensor")),
        P("batch", "tensor"),
        P(None, "grp"),
        P("grp"),
    )
    one_request = mesh.shape["batch"] == BEAMS and mesh.shape["tensor"] == 2
    return jax.shard_map(
        kernel_body if one_request else body,
        mesh=mesh,
        in_specs=placed,
        out_specs=(
            P(None, "grp", "batch"),
            P(None, ("grp", "batch"), "tensor"),
            P(("grp", "batch"), None, None, "tensor"),
        ),
        check_vma=False,
    )
```
